32 devices in a mesh: groups: 2 (over x), seq: 16 (over z, y, core).
Axes of the slice: x: 2, y: 2, z: 4, core: 2. Of those that a mesh axis runs over, the one named last changes fastest.
Arguments:
- streams: bfloat16 [32768, 3, 1024], P(('groups', 'seq')), parts along dimension 0, may hold values from -6 to 6
- short_filter: float32 [3, 3, 1024], replicated, may hold values from -3.5 to 3.5
- residues: float32 [16, 1024], replicated, may hold values from -1.5 to 1.5
- rates: float32 [16, 1024], replicated, may hold values from 6.1035157e-06 to 0.05
- skip: float32 [1024], replicated, may hold values from -1 to 1
Outputs:
- mixed: float32 [32768, 1024], P(('groups', 'seq')), parts along dimension 0
The draws below stay inside these ranges and needn't reach their ends.
There are 2 independent parts, one for each index of `groups`. The reference program is written for one: setup_inputs(seed, part) draws one part's arguments, and reference() takes and returns one part's arrays. A program takes and returns all parts, laid end to end along the dimension named above; an argument that names none is the same for every part. Nothing has to cross between parts.
All inputs are finite; a program needn't handle non-finite values.
Results may differ from the reference program's by a relative error of at most 0.0003.
Values may be sent and summed in bfloat16 or wider, within the bound.
No kernel may reach another device: no remote copies, remote signals or barrier semaphores. Data moves between devices by JAX's collectives and lax.ppermute only.
A program may use at most 192 MiB of HBM per device.

```python
import math
import jax
import jax.numpy as jnp
from jax import lax

CH = 1024
ORDER = 16
SHORT = 3
TOKENS = 16384


def shard_levels(stream_key, shape, pieces, least, high):
    def one(position, shards_of):
        heights = jax.random.uniform(jax.random.fold_in(jax.random.fold_in(stream_key, 6), position), (shards_of,), jnp.float32, least / len(pieces), high / len(pieces))
        return jnp.repeat(jnp.exp(heights), shape[position] // shards_of).reshape((-1,) + (1,) * (len(shape) - position - 1))

    loudness = one(*pieces[0])
    for cut in pieces[1:]:
        loudness = loudness * one(*cut)
    return loudness


def scatter_about(key, shape, width, most, split=(), held_as=jnp.bfloat16):
    drawn = jax.random.normal(key, shape, jnp.float32) * width
    if len(split) > 0:
        drawn = shard_levels(key, shape, split, -0.22, 0.18) * drawn
    return jnp.clip(drawn, min=-most, max=most).astype(held_as)


def setup_inputs(seed: int = 0, part: int = 0) -> dict:
    streams_of = jax.random.split(jax.random.key(seed), 6)
    part_splits = jax.random.split(jax.random.fold_in(streams_of[5], part), 6)
    return {
        "streams": scatter_about(part_splits[0], (TOKENS, 3, CH), 1.0, 6.0, ((0, 16),)),
        "short_filter": scatter_about(streams_of[1], (SHORT, 3, CH), SHORT ** -0.5, 3.5, (), jnp.float32),
        "residues": scatter_about(streams_of[2], (ORDER, CH), ORDER ** -0.5, 1.5, (), jnp.float32),
        "rates": jnp.clip(jnp.exp(jax.random.uniform(streams_of[3], (ORDER, CH), jnp.float32, math.log(6.10351571594947e-06), math.log(0.05))), 6.10351571594947e-06, 0.05),
        "skip": jnp.clip(jax.random.uniform(streams_of[4], (CH,), jnp.float32, -1.0, 1.0), -1.0, 1.0),
    }


def reference(streams, short_filter, residues, rates, skip):
    values_f32 = streams.astype(jnp.float32)
    tok_total = values_f32.shape[0]
    tap_count = short_filter.shape[0]
    padded = jnp.pad(values_f32, ((tap_count - 1, 0), (0, 0), (0, 0)))
    filtered = short_filter[0][None] * padded[tap_count - 1:tap_count - 1 + tok_total]
    for offset in range(1, tap_count):
        filtered = filtered + short_filter[offset][None] * padded[tap_count - 1 - offset:tap_count - 1 - offset + tok_total]
    queries = filtered[:, 0]
    gated_in = filtered[:, 1] * filtered[:, 2]
    coefficient = residues * jnp.sqrt(-jnp.expm1(-2.0 * rates))
    decays = jnp.exp(-rates)

    def advance(carried, drive):
        carried = decays * carried + drive[None]
        return (carried, lax.optimization_barrier(jnp.sum(coefficient * carried, axis=0)))
    _, convolved = lax.scan(advance, jnp.zeros_like(rates), gated_in)
    return queries * (convolved + skip[None] * gated_in)
```

```python
import functools

import jax
import jax.numpy as jnp
from jax import lax
from jax.experimental import pallas as pl
from jax.experimental.pallas import tpu as pltpu
from jax.sharding import PartitionSpec as P

SEG = 8
LANES = 128
PAD = 8
UNROLL = 8
f32 = jnp.float32


def rows(vec):
    return jnp.broadcast_to(vec, (SEG, LANES))


def total(parts):
    while len(parts) > 1:
        tail = [parts[-1]] if len(parts) % 2 else []
        parts = [a + b for a, b in zip(parts[::2], parts[1::2])] + tail
    return parts[0]


def later(x, by, fill):
    row = lax.broadcasted_iota(jnp.int32, x.shape, 0)
    return jnp.where(row >= by, pltpu.roll(x, by, 0), fill)


def spread(src, dst, steps):
    def one(i, _):
        here = pl.ds(pl.multiple_of(i * steps, 16), steps)
        there = pl.ds(pl.multiple_of(i * (steps + PAD), 8), steps)
        dst[there, :] = src[here, :].astype(f32)
        return 0

    lax.fori_loop(0, SEG, one, 0)
    return lambda k: dst[pl.ds(k, SEG, stride=steps + PAD), :]


def scan_steps(steps, one, start):
    def some(b, c):
        for u in range(UNROLL):
            c = one(b * UNROLL + u, c)
        return c

    return lax.fori_loop(0, steps // UNROLL, some, start)


def states_kernel(key_ref, val_ref, rim_ref, tap_ref, rate_ref, gated_ref, start_ref, end_ref, keys, vals):
    steps = key_ref.shape[0] // SEG
    modes = rate_ref.shape[0]
    at = [spread(key_ref, keys, steps), spread(val_ref, vals, steps)]
    taps = [[rows(tap_ref[d, j : j + 1, :]) for d in range(3)] for j in (1, 2)]
    decay = [rows(jnp.exp(-rate_ref[n : n + 1, :])) for n in range(modes)]
    before = []
    for j in range(2):
        before.append(later(at[j](steps - 1), 1, rim_ref[j + 1, 1:2, :]))
        before.append(later(at[j](steps - 2), 1, rim_ref[j + 1, 0:1, :]))

    def one(k, c):
        k1, k2, v1, v2, *state = c
        k0, v0 = at[0](k), at[1](k)
        a = taps[0][0] * k0 + taps[0][1] * k1 + taps[0][2] * k2
        b = taps[1][0] * v0 + taps[1][1] * v1 + taps[1][2] * v2
        x = a * b
        gated_ref[k] = x
        return (k0, k1, v0, v1, *[d * s + x for d, s in zip(decay, state)])

    zero = jnp.zeros((SEG, LANES), f32)
    final = scan_steps(steps, one, (*before, *[zero] * modes))[4:]
    for n in range(modes):
        s = final[n]
        d = rows(jnp.exp(-rate_ref[n : n + 1, :] * steps))
        for by in (1, 2, 4):
            s = s + d * later(s, by, 0.0)
            d = d * d
        start_ref[n] = later(s, 1, 0.0)
        end_ref[n : n + 1, :] = s[SEG - 1 : SEG, :]


def local_kernel(query_ref, gated_ref, rim_ref, tap_ref, rate_ref, coef_ref, skip_ref, start_ref, conv_ref, gate_ref, queries):
    steps = query_ref.shape[0] // SEG
    modes = rate_ref.shape[0]
    at = spread(query_ref, queries, steps)
    taps = [rows(tap_ref[d, 0:1, :]) for d in range(3)]
    decay = [rows(jnp.exp(-rate_ref[n : n + 1, :])) for n in range(modes)]
    coef = [rows(coef_ref[n : n + 1, :]) for n in range(modes)]
    skip = rows(skip_ref[...])
    before = (later(at(steps - 1), 1, rim_ref[0, 1:2, :]), later(at(steps - 2), 1, rim_ref[0, 0:1, :]))

    def one(k, c):
        q1, q2, *state = c
        q0, x = at(k), gated_ref[k]
        gate_ref[k] = taps[0] * q0 + taps[1] * q1 + taps[2] * q2
        state = [d * s + x for d, s in zip(decay, state)]
        conv_ref[k] = total([a * s for a, s in zip(coef, state)] + [skip * x])
        return (q0, q1, *state)

    scan_steps(steps, one, (*before, *[start_ref[n] for n in range(modes)]))


def carry_kernel(conv_ref, gate_ref, rate_ref, carry_ref, out_ref, mixed):
    steps = conv_ref.shape[0]
    modes = rate_ref.shape[0]
    decay = [rows(jnp.exp(-rate_ref[n : n + 1, :])) for n in range(modes)]
    first = lax.broadcasted_iota(jnp.int32, (SEG, LANES), 0).astype(f32) * steps
    part = [jnp.exp(-rate_ref[n : n + 1, :] * first) * carry_ref[n : n + 1, :] for n in range(modes)]

    def one(k, part):
        part = [d * s for d, s in zip(decay, part)]
        mixed[pl.ds(k, SEG, stride=steps + PAD), :] = gate_ref[k] * (conv_ref[k] + total(part))
        return part

    scan_steps(steps, one, part)

    def gather(i, _):
        there = pl.ds(pl.multiple_of(i * (steps + PAD), 8), steps)
        out_ref[pl.ds(pl.multiple_of(i * steps, 8), steps), :] = mixed[there, :]
        return 0

    lax.fori_loop(0, SEG, gather, 0)


def body(streams, short_filter, residues, rates, skip):
    tokens, _, channels = streams.shape
    modes = rates.shape[0]
    steps = tokens // SEG
    count, mine = lax.axis_size("seq"), lax.axis_index("seq")
    assert count & (count - 1) == 0 and tokens % (SEG * 16) == 0

    rim = lax.ppermute(streams[tokens - 2 :], "seq", [(i, i + 1) for i in range(count - 1)])
    rim = jnp.transpose(rim, (1, 0, 2)).astype(f32)
    by_stream = jnp.transpose(streams, (1, 0, 2))
    coefficient = residues * jnp.sqrt(-jnp.expm1(-2.0 * rates))

    def stream(j):
        return pl.BlockSpec((None, tokens, LANES), lambda c: (j, 0, c))

    grid = (channels // LANES,)
    segs = pl.BlockSpec((steps, SEG, LANES), lambda c: (0, 0, c))
    rims = pl.BlockSpec((3, 2, LANES), lambda c: (0, 0, c))
    taps = pl.BlockSpec((3, 3, LANES), lambda c: (0, 0, c))
    mode = pl.BlockSpec((modes, LANES), lambda c: (0, c))
    mode_segs = pl.BlockSpec((modes, SEG, LANES), lambda c: (0, 0, c))
    padded = pltpu.VMEM((SEG * (steps + PAD), LANES), f32)
    seg_shape = jax.ShapeDtypeStruct((steps, SEG, channels), f32)

    gated, starts, end = pl.pallas_call(
        states_kernel,
        grid=grid,
        in_specs=[stream(1), stream(2), rims, taps, mode],
        out_specs=[segs, mode_segs, mode],
        out_shape=[
            seg_shape,
            jax.ShapeDtypeStruct((modes, SEG, channels), f32),
            jax.ShapeDtypeStruct((modes, channels), f32),
        ],
        scratch_shapes=[padded, padded],
        name="states",
    )(by_stream, by_stream, rim, short_filter, rates)

    block, entering = end, jnp.zeros_like(end)
    size = 1
    while size < count:
        other = lax.ppermute(block, "seq", [(i, i ^ size) for i in range(count)])
        second = (mine & size) != 0
        behind = (mine & (size - 1)).astype(f32) * tokens
        entering = jnp.where(second, entering + jnp.exp(-rates * behind) * other, entering)
        across = jnp.exp(-rates * float(tokens * size))
        block = jnp.where(second, block + across * other, other + across * block)
        size *= 2

    conv, gate = pl.pallas_call(
        local_kernel,
        grid=grid,
        in_specs=[stream(0), segs, rims, taps, mode, mode, pl.BlockSpec((1, LANES), lambda c: (0, c)), mode_segs],
        out_specs=[segs, segs],
        out_shape=[seg_shape, seg_shape],
        scratch_shapes=[padded],
        name="local",
    )(by_stream, gated, rim, short_filter, rates, coefficient, skip[None], starts)

    return pl.pallas_call(
        carry_kernel,
        grid=grid,
        in_specs=[segs, segs, mode, mode],
        out_specs=pl.BlockSpec((tokens, LANES), lambda c: (0, c)),
        out_shape=jax.ShapeDtypeStruct((tokens, channels), f32),
        scratch_shapes=[padded],
        name="carry",
    )(conv, gate, rates, coefficient * entering)


def solution(mesh):
    placed = (P(("groups", "seq"), None, None), P(), P(), P(), P())
    return jax.shard_map(
        body, mesh=mesh, in_specs=placed, out_specs=P(("groups", "seq"), None), check_vma=False
    )
```

```python
import functools

import jax
import jax.numpy as jnp
from jax import lax
from jax.experimental import pallas as pl
from jax.experimental.pallas import tpu as pltpu
from jax.sharding import PartitionSpec as P


SEG = 8
LANES = 128
CHUNK = 16
PITCH = CHUNK + 8
VMEM_LIMIT = 16 << 20
f32 = jnp.float32


def rows(vec):
    return jnp.broadcast_to(vec, (SEG, LANES))


def total(parts):
    while len(parts) > 1:
        tail = [parts[-1]] if len(parts) % 2 else []
        parts = [a + b for a, b in zip(parts[::2], parts[1::2])] + tail
    return parts[0]


def later(x, by):
    row = lax.broadcasted_iota(jnp.int32, x.shape, 0)
    return jnp.where(row >= by, pltpu.roll(x, by, 0), 0.0)


def decays(rate_ref, times):
    return [rows(jnp.exp(-rate_ref[n : n + 1, :] * times)) for n in range(rate_ref.shape[0])]


class Spread:
    def __init__(self, block, slots, steps):
        self.block, self.slots, self.steps = block, slots, steps

    def load(self, seg, chunk, slot):
        start = pl.multiple_of(seg * self.steps + chunk * CHUNK, CHUNK)
        piece = self.block[pl.ds(start, CHUNK), :].astype(f32)
        self.slots[slot, pl.ds(seg * PITCH, CHUNK), :] = piece

    def load_all(self, chunk, slot):
        for seg in range(SEG):
            self.load(seg, chunk, slot)

    def at(self, slot, k):
        return self.slots[slot, pl.ds(k, SEG, stride=PITCH), :]


def chunk_loop(steps, one, ahead, start):
    chunks = steps // CHUNK

    def trip(b, c):
        slot, after = lax.rem(b, 2), lax.rem(b + 1, 2)
        coming = lax.rem(b + 1, chunks)
        for u in range(CHUNK):
            c = one(b * CHUNK + u, slot, u, c)
            ahead(u, b, coming, after)
        return c

    return lax.fori_loop(0, chunks, trip, start)


def states_kernel(key_ref, val_ref, tap_ref, rate_ref, gated_ref, start_ref, end_ref, key_slots, val_slots):
    steps = key_ref.shape[0] // SEG
    modes = rate_ref.shape[0]
    keys, vals = Spread(key_ref, key_slots, steps), Spread(val_ref, val_slots, steps)
    taps = [[rows(tap_ref[d, j : j + 1, :]) for d in range(3)] for j in (1, 2)]
    decay = decays(rate_ref, 1.0)
    before = []
    for part in (keys, vals):
        part.load_all(steps // CHUNK - 1, 1)
        part.load_all(0, 0)
        before += [later(part.at(1, CHUNK - 1), 1), later(part.at(1, CHUNK - 2), 1)]

    def one(k, slot, u, c):
        k1, k2, v1, v2, *state = c
        k0, v0 = keys.at(slot, u), vals.at(slot, u)
        a = taps[0][0] * k0 + taps[0][1] * k1 + taps[0][2] * k2
        b = taps[1][0] * v0 + taps[1][1] * v1 + taps[1][2] * v2
        x = a * b
        gated_ref[k] = x
        return (k0, k1, v0, v1, *[d * s + x for d, s in zip(decay, state)])

    def ahead(u, b, coming, after):
        (keys, vals)[u % 2].load(u // 2, coming, after)

    zero = jnp.zeros((SEG, LANES), f32)
    final = chunk_loop(steps, one, ahead, (*before, *[zero] * modes))[4:]
    for n, d in enumerate(decays(rate_ref, float(steps))):
        s = final[n]
        for by in (1, 2, 4):
            s = s + d * later(s, by)
            d = d * d
        start_ref[n] = later(s, 1)
        end_ref[n : n + 1, :] = s[SEG - 1 : SEG, :]


def edge_kernel(tokens, rim_ref, head_ref, tap_ref, rate_ref, end_ref, block_ref, change_ref):
    r0, r1 = [[rim_ref[t, j : j + 1, :].astype(f32) for j in range(3)] for t in range(2)]
    h0, h1 = [[head_ref[j, t : t + 1, :].astype(f32) for j in range(3)] for t in range(2)]
    w0, w1, w2 = [[tap_ref[d, j : j + 1, :] for j in range(3)] for d in range(3)]
    more0 = [w1[j] * r1[j] + w2[j] * r0[j] for j in range(3)]
    more1 = [w2[j] * r1[j] for j in range(3)]
    own0 = [w0[j] * h0[j] for j in range(3)]
    own1 = [w0[j] * h1[j] + w1[j] * h0[j] for j in range(3)]
    change0 = (own0[1] + more0[1]) * (own0[2] + more0[2]) - own0[1] * own0[2]
    change1 = (own1[1] + more1[1]) * (own1[2] + more1[2]) - own1[1] * own1[2]
    for i, row in enumerate((change0, change1, more0[0], more1[0])):
        change_ref[i : i + 1, :] = row
    rate = rate_ref[...]
    block_ref[...] = end_ref[...] + jnp.exp(-rate * (tokens - 1.0)) * change0 + jnp.exp(-rate * (tokens - 2.0)) * change1


def local_kernel(query_ref, gated_ref, tap_ref, rate_ref, coef_ref, skip_ref, start_ref, *rest):
    conv_ref, gate_ref, slots = rest[-3:]
    steps = query_ref.shape[0] // SEG
    modes = rate_ref.shape[0]
    queries = Spread(query_ref, slots, steps)
    taps = [rows(tap_ref[d, 0:1, :]) for d in range(3)]
    decay = decays(rate_ref, 1.0)
    coef = [rows(coef_ref[n : n + 1, :]) for n in range(modes)]
    skip = rows(skip_ref[...])
    queries.load_all(steps // CHUNK - 1, 1)
    queries.load_all(0, 0)
    before = (later(queries.at(1, CHUNK - 1), 1), later(queries.at(1, CHUNK - 2), 1))

    def one(k, slot, u, c):
        q1, q2, *state = c
        q0, x = queries.at(slot, u), gated_ref[k]
        gate_ref[k] = taps[0] * q0 + taps[1] * q1 + taps[2] * q2
        state = [d * s + x for d, s in zip(decay, state)]
        conv_ref[k] = total([a * s for a, s in zip(coef, state)] + [skip * x])
        return (q0, q1, *state)

    def ahead(u, b, coming, after):
        if u % 2 == 0:
            queries.load(u // 2, coming, after)

    chunk_loop(steps, one, ahead, (*before, *[start_ref[n] for n in range(modes)]))


def carry_kernel(
    conv_ref, gate_ref, rate_ref, coef_ref, skip_ref, enter_ref, change_ref, out_ref, slots
):
    steps = conv_ref.shape[0]
    modes = rate_ref.shape[0]
    decay = decays(rate_ref, 1.0)
    first = lax.broadcasted_iota(jnp.int32, (SEG, LANES), 0).astype(f32) * steps
    change = [change_ref[0:1, :], change_ref[1:2, :]]
    grow = jnp.exp(rate_ref[...])
    entering = coef_ref[...] * (enter_ref[...] + grow * (change[0] + grow * change[1]))
    part = [jnp.exp(-rate_ref[n : n + 1, :] * first) * entering[n : n + 1, :] for n in range(modes)]

    def one(k, slot, u, part):
        part = [d * s for d, s in zip(decay, part)]
        slots[slot, pl.ds(u, SEG, stride=PITCH), :] = gate_ref[k] * (conv_ref[k] + total(part))
        return part

    def put(seg, chunk, slot):
        start = pl.multiple_of(seg * steps + chunk * CHUNK, CHUNK)
        out_ref[pl.ds(start, CHUNK), :] = slots[slot, pl.ds(seg * PITCH, CHUNK), :]

    def ahead(u, b, coming, after):
        if u % 2 == 0:
            put(u // 2, jnp.maximum(b - 1, 0), after)

    chunk_loop(steps, one, ahead, part)
    chunks = steps // CHUNK
    for seg in range(SEG):
        put(seg, chunks - 1, (chunks - 1) % 2)

    decay = jnp.exp(-rate_ref[...])
    skip = skip_ref[...]
    from0 = jnp.sum(entering * decay - coef_ref[...] * (grow * change[1]), axis=0, keepdims=True)
    from1 = jnp.sum(entering * (decay * decay), axis=0, keepdims=True)
    gate0 = gate_ref[0, 0:1, :] + change_ref[2:3, :]
    gate1 = gate_ref[1, 0:1, :] + change_ref[3:4, :]
    out_ref[0:1, :] = gate0 * (conv_ref[0, 0:1, :] + skip * change[0] + from0)
    out_ref[1:2, :] = gate1 * (conv_ref[1, 0:1, :] + skip * change[1] + from1)


def in_hbm(x):
    return pltpu.with_memory_space_constraint(x, pltpu.HBM)


def windows(groups, rounds):
    counts = [0] * rounds
    order = [*range(1, rounds), 0]
    for i in range(groups):
        counts[order[i % rounds]] += 1
    return counts


def body(streams, short_filter, residues, rates, skip):
    tokens, _, channels = streams.shape
    modes = rates.shape[0]
    steps = tokens // SEG
    groups = channels // LANES
    count, mine = lax.axis_size("seq"), lax.axis_index("seq")
    assert count & (count - 1) == 0 and tokens % (SEG * CHUNK * 2) == 0

    by_stream = in_hbm(jnp.transpose(streams, (1, 0, 2)))
    apart = lax.optimization_barrier(rates)
    coefficient = lax.optimization_barrier(residues * jnp.sqrt(-jnp.expm1(-2.0 * apart)))
    skip = skip[None]

    def stream(j, at):
        return pl.BlockSpec((None, tokens, LANES), lambda c: (j, 0, c + at))

    def cols(*shape, at=0):
        return pl.BlockSpec((*shape, LANES), lambda c: (*[0] * len(shape), c + at))

    segs_shape = pltpu.HBM((steps, SEG, channels), f32)
    slots = pltpu.VMEM((2, SEG * PITCH, LANES), f32)
    anywhere = pl.BlockSpec(memory_space=pl.ANY)
    params = pltpu.CompilerParams(vmem_limit_bytes=VMEM_LIMIT)

    rim = lax.ppermute(streams[tokens - 2 :], "seq", [(i, i + 1) for i in range(count - 1)])

    gated, starts, end = pl.pallas_call(
        states_kernel,
        grid=(groups,),
        in_specs=[stream(1, 0), stream(2, 0), cols(3, 3), cols(modes)],
        out_specs=[cols(steps, SEG), cols(modes, SEG), cols(modes)],
        out_shape=[
            segs_shape,
            jax.ShapeDtypeStruct((modes, SEG, channels), f32),
            jax.ShapeDtypeStruct((modes, channels), f32),
        ],
        scratch_shapes=[slots, slots],
        compiler_params=params,
        name="states",
    )(by_stream, by_stream, short_filter, rates)

    end, change = pl.pallas_call(
        functools.partial(edge_kernel, tokens),
        grid=(1,),
        in_specs=[
            pl.BlockSpec((2, 3, channels), lambda i: (0, 0, 0)),
            pl.BlockSpec((3, CHUNK, channels), lambda i: (0, 0, 0)),
            pl.BlockSpec((3, 3, channels), lambda i: (0, 0, 0)),
            pl.BlockSpec((modes, channels), lambda i: (0, 0)),
            pl.BlockSpec((modes, channels), lambda i: (0, 0)),
        ],
        out_specs=[pl.BlockSpec((modes, channels), lambda i: (0, 0)), pl.BlockSpec((4, channels), lambda i: (0, 0))],
        out_shape=[jax.ShapeDtypeStruct((modes, channels), f32), jax.ShapeDtypeStruct((4, channels), f32)],
        compiler_params=params,
        name="edge",
    )(rim, by_stream, short_filter, rates, end)

    rounds = count.bit_length() - 1
    block, entering = end, jnp.zeros_like(end)
    made, at = (), 0
    for r, beside in enumerate(windows(groups, rounds)):
        size = 1 << r
        other = lax.ppermute(block, "seq", [(i, i ^ size) for i in range(count)])
        if beside:
            inputs = [by_stream, in_hbm(gated), short_filter, rates, coefficient, skip, starts]
            made = pl.pallas_call(
                local_kernel,
                grid=(beside,),
                in_specs=[
                    stream(0, at),
                    cols(steps, SEG, at=at),
                    cols(3, 3, at=at),
                    cols(modes, at=at),
                    cols(modes, at=at),
                    cols(1, at=at),
                    cols(modes, SEG, at=at),
                    *[anywhere] * len(made),
                ],
                out_specs=[cols(steps, SEG, at=at)] * 2,
                out_shape=[segs_shape, segs_shape],
                input_output_aliases={len(inputs) + i: i for i in range(len(made))},
                scratch_shapes=[slots],
                compiler_params=params,
        name="local",
            )(*inputs, *made)
            at += beside
        second = (mine & size) != 0
        behind = (mine & (size - 1)).astype(f32) * tokens
        entering = jnp.where(second, entering + jnp.exp(-rates * behind) * other, entering)
        across = jnp.exp(-rates * float(tokens * size))
        block = jnp.where(second, block + across * other, other + across * block)
    conv, gate = made

    return pl.pallas_call(
        carry_kernel,
        grid=(groups,),
        in_specs=[
            cols(steps, SEG),
            cols(steps, SEG),
            cols(modes),
            cols(modes),
            cols(1),
            cols(modes),
            cols(4),
        ],
        out_specs=cols(tokens),
        out_shape=pltpu.HBM((tokens, channels), f32),
        scratch_shapes=[slots],
        compiler_params=params,
        name="carry",
    )(in_hbm(conv), in_hbm(gate), rates, coefficient, skip, entering, change)


def solution(mesh):
    placed = (P(("groups", "seq"), None, None), P(), P(), P(), P())

    return jax.shard_map(
        body, mesh=mesh, in_specs=placed, out_specs=P(("groups", "seq"), None), check_vma=False
    )
```

```python
import functools

import jax
import jax.numpy as jnp
from jax import lax
from jax.experimental import pallas as pl
from jax.experimental.pallas import tpu as pltpu
from jax.sharding import PartitionSpec as P


SEG = 8
LANES = 128
CHUNK = 16
PITCH = CHUNK + 8
EDGE = 16
VMEM_LIMIT = 16 << 20
f32 = jnp.float32


def rows(vec):
    return jnp.broadcast_to(vec, (SEG, LANES))


def total(parts):
    while len(parts) > 1:
        tail = [parts[-1]] if len(parts) % 2 else []
        parts = [a + b for a, b in zip(parts[::2], parts[1::2])] + tail
    return parts[0]


def later(x, by):
    row = lax.broadcasted_iota(jnp.int32, x.shape, 0)
    return jnp.where(row >= by, pltpu.roll(x, by, 0), 0.0)


def each(ref, at):
    return [rows(ref[n : n + 1, at]) for n in range(ref.shape[0])]


class Spread:
    def __init__(self, block, slots, steps):
        self.block, self.slots, self.steps = block, slots, steps

    def load(self, seg, chunk, slot):
        start = pl.multiple_of(seg * self.steps + chunk * CHUNK, CHUNK)
        piece = self.block[pl.ds(start, CHUNK), :].astype(f32)
        self.slots[slot, pl.ds(seg, CHUNK, stride=SEG), :] = piece

    def load_all(self, chunk, slot):
        for seg in range(SEG):
            self.load(seg, chunk, slot)

    def at(self, slot, k):
        return self.slots[slot, pl.ds(k * SEG, SEG), :]


def chunk_loop(steps, one, ahead, start):
    chunks = steps // CHUNK

    def trip(b, c):
        slot, after = lax.rem(b, 2), lax.rem(b + 1, 2)
        coming = lax.rem(b + 1, chunks)
        for u in range(CHUNK):
            c = one(b * CHUNK + u, slot, u, c)
            ahead(u, b, coming, after)
        return c

    return lax.fori_loop(0, chunks, trip, start)


def lanes(c):
    return pl.ds(pl.multiple_of(c * LANES, LANES), LANES)


def states_kernel(
    stream_ref, tap_ref, rate_ref,
    gated_ref, start_ref, send_ref, query_ref, taps_ref, rates_ref, decay_ref, enter_ref,
    raw, head, stride_decay, key_slots, val_slots, raw_sem, query_sem, small_sem,
):
    groups, steps = gated_ref.shape[:2]
    modes, tokens = rate_ref.shape[0], steps * SEG

    def fetch(c, slot):
        return pltpu.make_async_copy(stream_ref.at[1:3, :, lanes(c)], raw.at[slot], raw_sem.at[slot])

    def fetch_query(c):
        return pltpu.make_async_copy(stream_ref.at[0, :, lanes(c)], query_ref.at[c], query_sem.at[c])

    small = [
        pltpu.make_async_copy(rate_ref, rates_ref, small_sem.at[0]),
        pltpu.make_async_copy(tap_ref, taps_ref, small_sem.at[1]),
        pltpu.make_async_copy(stream_ref.at[:, 0:CHUNK, :], head.at[0], small_sem.at[2]),
        pltpu.make_async_copy(stream_ref.at[:, pl.ds(tokens - CHUNK, CHUNK), :], head.at[1], small_sem.at[3]),
    ]
    fetch(0, 0).start()
    for copy in small:
        copy.start()
    for copy in small:
        copy.wait()
    decay_ref[...] = jnp.exp(-rates_ref[...])
    stride_decay[...] = jnp.exp(-rates_ref[...] * float(steps))
    enter_ref[...] = jnp.zeros_like(enter_ref)
    edge = [head[1, j, CHUNK - 2 :, :].astype(f32) for j in (1, 2, 0)] + [head[0, j, :2, :].astype(f32) for j in (1, 2)]
    for i, pair in enumerate(edge):
        send_ref[modes + 2 * i : modes + 2 * i + 2, :] = pair
    send_ref[modes + 2 * len(edge) :, :] = jnp.zeros((EDGE - 2 * len(edge), send_ref.shape[1]), f32)

    def group(c, _):
        slot = lax.rem(c, 2)

        @pl.when(c + 1 < groups)
        def _():
            fetch(c + 1, 1 - slot).start()

        fetch_query(c).start()
        fetch(c, slot).wait()
        keys = Spread(raw.at[slot, 0], key_slots, steps)
        vals = Spread(raw.at[slot, 1], val_slots, steps)
        at = lanes(c)
        taps = [[rows(taps_ref[d, j : j + 1, at]) for d in range(3)] for j in (1, 2)]
        decay = each(decay_ref, at)
        before = []
        for part in (keys, vals):
            part.load_all(steps // CHUNK - 1, 1)
            part.load_all(0, 0)
            before += [later(part.at(1, CHUNK - 1), 1), later(part.at(1, CHUNK - 2), 1)]

        def one(k, slot, u, carried):
            k1, k2, v1, v2, *state = carried
            k0, v0 = keys.at(slot, u), vals.at(slot, u)
            a = taps[0][0] * k0 + taps[0][1] * k1 + taps[0][2] * k2
            b = taps[1][0] * v0 + taps[1][1] * v1 + taps[1][2] * v2
            x = a * b
            gated_ref[c, k] = x
            return (k0, k1, v0, v1, *[d * s + x for d, s in zip(decay, state)])

        def ahead(u, b, coming, after):
            (keys, vals)[u % 2].load(u // 2, coming, after)

        zero = jnp.zeros((SEG, LANES), f32)
        final = chunk_loop(steps, one, ahead, (*before, *[zero] * modes))[4:]
        for n, d in enumerate(each(stride_decay, at)):
            s = final[n]
            for by in (1, 2, 4):
                s = s + d * later(s, by)
                d = d * d
            start_ref[c, n] = later(s, 1)
            send_ref[n : n + 1, at] = s[SEG - 1 : SEG, :]
        return 0

    lax.fori_loop(0, groups, group, 0)

    def landed(c, _):
        fetch_query(c).wait()
        return 0

    lax.fori_loop(0, groups, landed, 0)


def join_kernel(size, tokens, tap_ref, rate_ref, other_ref, mine_ref, enter_ref, enter_out, *mine_out):
    modes = rate_ref.shape[0]
    place = lax.axis_index("seq")
    second = (place & size) != 0
    rate = rate_ref[...]

    def after(times):
        return jnp.exp(-rate * times)

    def change(early, late):
        rim = [early[modes + i : modes + i + 1, :] for i in range(6)]
        head = [late[modes + i : modes + i + 1, :] for i in range(6, 10)]
        w = [[tap_ref[d, j : j + 1, :] for d in range(3)] for j in (1, 2, 0)]
        more0 = [w[j][1] * rim[2 * j + 1] + w[j][2] * rim[2 * j] for j in range(3)]
        more1 = [w[j][2] * rim[2 * j + 1] for j in range(3)]
        own0 = [w[j][0] * head[2 * j] for j in range(2)]
        own1 = [w[j][0] * head[2 * j + 1] + w[j][1] * head[2 * j] for j in range(2)]
        change0 = (own0[0] + more0[0]) * (own0[1] + more0[1]) - own0[0] * own0[1]
        change1 = (own1[0] + more1[0]) * (own1[1] + more1[1]) - own1[0] * own1[1]
        return change0, change1, more0[2], more1[2]

    def merge(early, late, out, change0, change1):
        span = float(tokens * size)
        out[:modes, :] = (
            late[:modes, :] + after(span) * early[:modes, :] + after(span - 1.0) * change0 + after(span - 2.0) * change1
        )
        out[modes : modes + 6, :] = late[modes : modes + 6, :]
        out[modes + 6 :, :] = early[modes + 6 :, :]

    @pl.when(second)
    def _():
        edge = change(other_ref, mine_ref)
        before = place & (size - 1)
        span = before.astype(f32) * float(tokens)
        enter_out[:modes, :] = (
            enter_ref[:modes, :]
            + after(span) * other_ref[:modes, :]
            + after(span - 1.0) * edge[0]
            + after(span - 2.0) * edge[1]
        )
        enter_out[modes:, :] = enter_ref[modes:, :]

        @pl.when(before == 0)
        def _():
            for i, row in enumerate(edge):
                enter_out[modes + i : modes + i + 1, :] = row

        if mine_out:
            merge(other_ref, mine_ref, mine_out[0], *edge[:2])

    @pl.when(jnp.logical_not(second))
    def _():
        enter_out[...] = enter_ref[...]
        if mine_out:
            merge(mine_ref, other_ref, mine_out[0], *change(mine_ref, other_ref)[:2])


def local_kernel(at, beside, query_ref, gated_ref, tap_ref, decay_ref, coef_ref, skip_ref, start_ref, *rest):
    conv_ref, gate_ref, slots = rest[-3:]
    steps = gated_ref.shape[1]
    modes = decay_ref.shape[0]

    def group(i, _):
        c = i + at
        on = lanes(c)
        queries = Spread(query_ref.at[c], slots, steps)
        taps = [rows(tap_ref[d, 0:1, on]) for d in range(3)]
        decay, coef = each(decay_ref, on), each(coef_ref, on)
        skip = rows(skip_ref[:, on])
        queries.load_all(steps // CHUNK - 1, 1)
        queries.load_all(0, 0)
        before = (later(queries.at(1, CHUNK - 1), 1), later(queries.at(1, CHUNK - 2), 1))

        def one(k, slot, u, carried):
            q1, q2, *state = carried
            q0, x = queries.at(slot, u), gated_ref[c, k]
            gate_ref[c, k] = taps[0] * q0 + taps[1] * q1 + taps[2] * q2
            state = [d * s + x for d, s in zip(decay, state)]
            conv_ref[c, k] = total([a * s for a, s in zip(coef, state)] + [skip * x])
            return (q0, q1, *state)

        def ahead(u, b, coming, after):
            if u % 2 == 0:
                queries.load(u // 2, coming, after)

        chunk_loop(steps, one, ahead, (*before, *[start_ref[c, n] for n in range(modes)]))
        return 0

    lax.fori_loop(0, beside, group, 0)


def carry_kernel(conv_ref, gate_ref, rate_ref, decay_ref, coef_ref, skip_ref, enter_ref, out_ref, mixed, slots, sem):
    groups, steps = conv_ref.shape[:2]
    modes, chunks = rate_ref.shape[0], steps // CHUNK

    def store(c, side):
        return pltpu.make_async_copy(mixed.at[side], out_ref.at[:, lanes(c)], sem.at[side])

    def group(c, _):
        side, on = lax.rem(c, 2), lanes(c)

        @pl.when(c >= 2)
        def _():
            store(c - 2, side).wait()

        rate, weight = rate_ref[:, on], coef_ref[:, on]
        decay = each(decay_ref, on)
        first = lax.broadcasted_iota(jnp.int32, (SEG, LANES), 0).astype(f32) * steps
        entering = weight * enter_ref[:modes, on]
        part = [jnp.exp(-rate[n : n + 1, :] * first) * entering[n : n + 1, :] for n in range(modes)]

        def one(k, slot, u, part):
            part = [d * s for d, s in zip(decay, part)]
            slots[slot, pl.ds(u, SEG, stride=PITCH), :] = gate_ref[c, k] * (conv_ref[c, k] + total(part))
            return part

        def put(seg, chunk, slot):
            start = pl.multiple_of(seg * steps + chunk * CHUNK, CHUNK)
            mixed[side, pl.ds(start, CHUNK), :] = slots[slot, pl.ds(seg * PITCH, CHUNK), :]

        def ahead(u, b, coming, after):
            if u % 2 == 0:
                put(u // 2, jnp.maximum(b - 1, 0), after)

        chunk_loop(steps, one, ahead, part)
        for seg in range(SEG):
            put(seg, chunks - 1, (chunks - 1) % 2)

        once = decay_ref[:, on]
        skip = skip_ref[:, on]
        change = [enter_ref[modes + i : modes + i + 1, on] for i in range(4)]
        from0 = jnp.sum(entering * once - weight * (jnp.exp(rate) * change[1]), axis=0, keepdims=True)
        from1 = jnp.sum(entering * (once * once), axis=0, keepdims=True)
        gate0 = gate_ref[c, 0, 0:1, :] + change[2]
        gate1 = gate_ref[c, 1, 0:1, :] + change[3]
        mixed[side, 0:1, :] = gate0 * (conv_ref[c, 0, 0:1, :] + skip * change[0] + from0)
        mixed[side, 1:2, :] = gate1 * (conv_ref[c, 1, 0:1, :] + skip * change[1] + from1)
        store(c, side).start()
        return 0

    lax.fori_loop(0, groups, group, 0)
    for c in range(max(groups - 2, 0), groups):
        store(c, c % 2).wait()


def in_hbm(x):
    return pltpu.with_memory_space_constraint(x, pltpu.HBM)


def windows(groups, rounds):
    counts = [0] * rounds
    order = [*range(1, rounds), 0]
    for i in range(groups):
        counts[order[i % rounds] if i < rounds else 1 + (i - rounds) % (rounds - 1)] += 1
    return counts


def body(streams, short_filter, residues, rates, skip):
    tokens, _, channels = streams.shape
    modes = rates.shape[0]
    steps = tokens // SEG
    groups = channels // LANES
    count = lax.axis_size("seq")
    assert count & (count - 1) == 0 and tokens % (SEG * CHUNK * 2) == 0

    by_stream = in_hbm(jnp.transpose(streams, (1, 0, 2)))
    apart = lax.optimization_barrier(rates)
    coefficient = lax.optimization_barrier(residues * jnp.sqrt(-jnp.expm1(-2.0 * apart)))
    skip = skip[None]

    segs = pltpu.VMEM((groups, steps, SEG, LANES), f32)
    spread = pltpu.VMEM((2, SEG * CHUNK, LANES), f32)
    slots = pltpu.VMEM((2, SEG * PITCH, LANES), f32)
    hbm = pl.BlockSpec(memory_space=pltpu.HBM)
    whole = pl.BlockSpec(memory_space=pltpu.VMEM)
    params = pltpu.CompilerParams(vmem_limit_bytes=VMEM_LIMIT)

    block_shape = pltpu.VMEM((modes + EDGE, channels), f32)
    enter_shape = pltpu.VMEM((modes + 4, channels), f32)
    mode_shape = pltpu.VMEM((modes, channels), f32)

    gated, starts, block, query, taps, rate, decay, entering = pl.pallas_call(
        states_kernel,
        in_specs=[hbm] * 3,
        out_specs=[whole] * 8,
        out_shape=[
            segs,
            pltpu.VMEM((groups, modes, SEG, LANES), f32),
            block_shape,
            pltpu.VMEM((groups, tokens, LANES), streams.dtype),
            pltpu.VMEM(short_filter.shape, f32),
            mode_shape,
            mode_shape,
            enter_shape,
        ],
        scratch_shapes=[
            pltpu.VMEM((2, 2, tokens, LANES), streams.dtype),
            pltpu.VMEM((2, 3, CHUNK, channels), streams.dtype),
            mode_shape,
            spread,
            spread,
            pltpu.SemaphoreType.DMA((2,)),
            pltpu.SemaphoreType.DMA((groups,)),
            pltpu.SemaphoreType.DMA((4,)),
        ],
        compiler_params=params,
        name="states",
    )(by_stream, in_hbm(short_filter), in_hbm(rates))

    rounds = count.bit_length() - 1
    made, at = (), 0
    for r, beside in enumerate(windows(groups, rounds)):
        size = 1 << r
        other = lax.ppermute(block, "seq", [(i, i ^ size) for i in range(count)])
        if beside:
            inputs = [query, gated, taps, decay, coefficient, skip, starts]
            made = pl.pallas_call(
                functools.partial(local_kernel, at, beside),
                in_specs=[whole] * len(inputs) + [whole] * len(made),
                out_specs=[whole] * 2,
                out_shape=[segs, segs],
                input_output_aliases={len(inputs) + i: i for i in range(len(made))},
                scratch_shapes=[spread],
                compiler_params=params,
                name="local",
            )(*inputs, *made)
            at += beside
        last = r == rounds - 1
        entering, *blocks = pl.pallas_call(
            functools.partial(join_kernel, size, tokens),
            in_specs=[whole] * 5,
            out_specs=[whole] * (1 if last else 2),
            out_shape=[enter_shape] if last else [enter_shape, block_shape],
            compiler_params=params,
            name="join",
        )(taps, rate, other, block, entering)
        block = None if last else blocks[0]
    conv, gate = made

    return pl.pallas_call(
        carry_kernel,
        in_specs=[whole] * 7,
        out_specs=hbm,
        out_shape=pltpu.HBM((tokens, channels), f32),
        scratch_shapes=[pltpu.VMEM((2, tokens, LANES), f32), slots, pltpu.SemaphoreType.DMA((2,))],
        compiler_params=params,
        name="carry",
    )(conv, gate, rate, decay, coefficient, skip, entering)


def solution(mesh):
    placed = (P(("groups", "seq"), None, None), P(), P(), P(), P())

    return jax.shard_map(body, mesh=mesh, in_specs=placed, out_specs=P(("groups", "seq"), None), check_vma=False)
```

```python
import functools

import jax
import jax.numpy as jnp
from jax import lax
from jax.experimental import pallas as pl
from jax.experimental.pallas import tpu as pltpu
from jax.sharding import PartitionSpec as P


SEG = 8
LANES = 128
CHUNK = 32
TILE = 16
RIM, HEAD = 6, 4
PITCH = CHUNK + 8
VMEM_LIMIT = 16 << 20
f32 = jnp.float32


def rows(vec):
    return jnp.broadcast_to(vec, (SEG, LANES))


def total(parts):
    while len(parts) > 1:
        tail = [parts[-1]] if len(parts) % 2 else []
        parts = [a + b for a, b in zip(parts[::2], parts[1::2])] + tail
    return parts[0]


def later(x, by):
    row = lax.broadcasted_iota(jnp.int32, x.shape, 0)
    return jnp.where(row >= by, pltpu.roll(x, by, 0), 0.0)


def each(ref, at):
    return [rows(ref[n : n + 1, at]) for n in range(ref.shape[0])]


class Spread:
    def __init__(self, block, slots, steps):
        self.block, self.slots, self.steps = block, slots, steps

    def load(self, seg, chunk, slot, tile, first=0):
        start = pl.multiple_of(seg * self.steps + chunk * CHUNK + tile * TILE, TILE)
        piece = self.block[pl.ds(start, TILE), :].astype(f32)[first:]
        self.slots[slot, pl.ds((tile * TILE + first) * SEG + seg, TILE - first, stride=SEG), :] = piece

    def at(self, slot, k):
        return self.slots[slot, pl.ds(k * SEG, SEG), :]

    def begin(self):
        tiles = CHUNK // TILE
        for seg in range(SEG):
            self.load(seg, self.steps // CHUNK - 1, 1, tiles - 1, TILE - 2)
            for tile in range(tiles):
                self.load(seg, 0, 0, tile)
        return later(self.at(1, CHUNK - 1), 1), later(self.at(1, CHUNK - 2), 1)


def spreading(parts):
    items = [(p, seg, tile) for tile in range(CHUNK // TILE) for seg in range(SEG) for p in parts]

    def ahead(u, b, coming, after):
        for p, seg, tile in items[u * len(items) // CHUNK : (u + 1) * len(items) // CHUNK]:
            p.load(seg, coming, after, tile)

    return ahead


def chunk_loop(steps, one, ahead, start):
    chunks = steps // CHUNK

    def trip(b, c):
        slot, after = lax.rem(b, 2), lax.rem(b + 1, 2)
        coming = lax.rem(b + 1, chunks)
        for u in range(CHUNK):
            c = one(b * CHUNK + u, slot, u, c)
            ahead(u, b, coming, after)
        return c

    return lax.fori_loop(0, chunks, trip, start)


def lanes(c):
    return pl.ds(pl.multiple_of(c * LANES, LANES), LANES)


def states_kernel(
    stream_ref, tap_ref, rate_ref,
    gated_ref, start_ref, send_ref, query_ref, taps_ref, tall_taps, tall_rates, rates_ref, decay_ref, enter_ref,
    raw, stride_decay, key_slots, val_slots, raw_sem, query_sem, small_sem,
):
    groups, steps = gated_ref.shape[:2]
    modes, tokens = rate_ref.shape[0], steps * SEG

    def fetch(c, slot):
        return pltpu.make_async_copy(stream_ref.at[1:3, :, lanes(c)], raw.at[slot], raw_sem.at[slot])

    def fetch_query(c):
        return pltpu.make_async_copy(stream_ref.at[0, :, lanes(c)], query_ref.at[c], query_sem.at[c])

    small = [
        pltpu.make_async_copy(rate_ref, rates_ref, small_sem.at[0]),
        pltpu.make_async_copy(tap_ref, taps_ref, small_sem.at[1]),
    ]
    fetch(0, 0).start()
    for copy in small:
        copy.start()
    for copy in small:
        copy.wait()
    decay_ref[...] = jnp.exp(-rates_ref[...])
    stride_decay[...] = jnp.exp(-rates_ref[...] * float(steps))
    enter_ref[...] = jnp.zeros_like(enter_ref)

    def group(c, _):
        slot = lax.rem(c, 2)

        @pl.when(c + 1 < groups)
        def _():
            fetch(c + 1, 1 - slot).start()

        fetch_query(c).start()
        fetch(c, slot).wait()
        keys = Spread(raw.at[slot, 0], key_slots, steps)
        vals = Spread(raw.at[slot, 1], val_slots, steps)
        at, row = lanes(c), pl.ds(c, 1)
        taps = [[rows(taps_ref[d, j : j + 1, at]) for d in range(3)] for j in (1, 2)]
        decay = each(decay_ref, at)
        before = [*keys.begin(), *vals.begin()]

        def one(k, slot, u, carried):
            k1, k2, v1, v2, *state = carried
            k0, v0 = keys.at(slot, u), vals.at(slot, u)
            a = taps[0][0] * k0 + taps[0][1] * k1 + taps[0][2] * k2
            b = taps[1][0] * v0 + taps[1][1] * v1 + taps[1][2] * v2
            x = a * b
            gated_ref[c, k] = x
            return (k0, k1, v0, v1, *[d * s + x for d, s in zip(decay, state)])

        zero = jnp.zeros((SEG, LANES), f32)
        final = chunk_loop(steps, one, spreading((keys, vals)), (*before, *[zero] * modes))[4:]
        for n, d in enumerate(each(stride_decay, at)):
            s = final[n]
            for by in (1, 2, 4):
                s = s + d * later(s, by)
                d = d * d
            start_ref[c, n] = later(s, 1)
            send_ref[n, row, :] = s[SEG - 1 : SEG, :]
            tall_rates[n, row, :] = rates_ref[n : n + 1, at]
        for j in range(3):
            for d in range(3):
                tall_taps[3 * j + d, row, :] = taps_ref[d, j : j + 1, at]
        for j in range(2):
            rim = raw[slot, j, tokens - TILE :, :].astype(f32)[TILE - 2 :]
            head = raw[slot, j, :TILE, :].astype(f32)[:2]
            for t in range(2):
                send_ref[modes + 2 * j + t, row, :] = rim[t : t + 1]
                send_ref[modes + RIM + 2 * j + t, row, :] = head[t : t + 1]
                enter_ref[modes + 4 + 2 * j + t, row, :] = head[t : t + 1]
        return 0

    lax.fori_loop(0, groups, group, 0)

    def landed(c, _):
        fetch_query(c).wait()
        rim = query_ref[c, tokens - TILE :, :].astype(f32)[TILE - 2 :]
        for t in range(2):
            send_ref[modes + 4 + t, pl.ds(c, 1), :] = rim[t : t + 1]
        return 0

    lax.fori_loop(0, groups, landed, 0)


def join_kernel(size, tokens, last, tap_ref, rate_ref, coef_ref, skip_ref, other_ref, mine_ref, enter_ref, enter_out, *mine_out):
    modes = rate_ref.shape[0]
    rim_at, change_at, head_at = modes, modes, modes + 4
    place = lax.axis_index("seq")
    second = (place & size) != 0
    rate = rate_ref[...]

    def after(times):
        return jnp.exp(-rate * times)

    def change(rim, head):
        w = [[tap_ref[3 * j + d] for d in range(3)] for j in (1, 2, 0)]
        more0 = [w[j][1] * rim[2 * j + 1] + w[j][2] * rim[2 * j] for j in range(3)]
        more1 = [w[j][2] * rim[2 * j + 1] for j in range(3)]
        own0 = [w[j][0] * head[2 * j] for j in range(2)]
        own1 = [w[j][0] * head[2 * j + 1] + w[j][1] * head[2 * j] for j in range(2)]
        change0 = (own0[0] + more0[0]) * (own0[1] + more0[1]) - own0[0] * own0[1]
        change1 = (own1[0] + more1[0]) * (own1[1] + more1[1]) - own1[0] * own1[1]
        return change0, change1, more0[2], more1[2]

    def merge(early, late, change0, change1, head_ref, head_from):
        span = float(tokens * size)
        out = mine_out[0]
        out[:modes] = late[:modes] + after(span) * early[:modes] + after(span - 1.0) * change0 + after(span - 2.0) * change1
        out[rim_at : rim_at + RIM] = late[rim_at : rim_at + RIM]
        head = head_ref[head_from : head_from + HEAD]
        enter_out[head_at : head_at + HEAD] = head
        if out.shape[0] > modes + RIM:
            out[rim_at + RIM :] = head

    @pl.when(second)
    def _():
        edge = change(other_ref[rim_at : rim_at + RIM], enter_ref[head_at : head_at + HEAD])
        before = place & (size - 1)
        span = before.astype(f32) * float(tokens)
        enter_out[:modes] = (
            enter_ref[:modes] + after(span) * other_ref[:modes] + after(span - 1.0) * edge[0] + after(span - 2.0) * edge[1]
        )
        enter_out[change_at:] = enter_ref[change_at:]

        @pl.when(before == 0)
        def _():
            for i, row in enumerate(edge):
                enter_out[change_at + i] = row

        if not last:
            merge(other_ref, mine_ref, *edge[:2], other_ref, rim_at + RIM)

    @pl.when(jnp.logical_not(second))
    def _():
        enter_out[...] = enter_ref[...]
        if not last:
            edge = change(mine_ref[rim_at : rim_at + RIM], other_ref[rim_at + RIM : rim_at + RIM + HEAD])
            merge(mine_ref, other_ref, *edge[:2], enter_ref, head_at)

    if last:
        coef, skip = coef_ref[...], skip_ref[0]
        weight = coef * enter_out[:modes]
        change0, change1 = enter_out[change_at], enter_out[change_at + 1]
        once = after(1.0)
        enter_out[:modes] = weight
        enter_out[change_at] = skip * change0 + jnp.sum(weight * once - coef * (after(-1.0) * change1), axis=0)
        enter_out[change_at + 1] = skip * change1 + jnp.sum(weight * (once * once), axis=0)


def local_kernel(at, beside, query_ref, gated_ref, tap_ref, decay_ref, coef_ref, skip_ref, start_ref, *rest):
    conv_ref, gate_ref, slots = rest[-3:]
    steps = gated_ref.shape[1]
    modes = decay_ref.shape[0]

    def group(i, _):
        c = i + at
        on = lanes(c)
        queries = Spread(query_ref.at[c], slots, steps)
        taps = [rows(tap_ref[d, 0:1, on]) for d in range(3)]
        decay = each(decay_ref, on)
        coef = [rows(coef_ref[n, pl.ds(c, 1), :]) for n in range(modes)]
        skip = rows(skip_ref[0, pl.ds(c, 1), :])
        before = queries.begin()

        def one(k, slot, u, carried):
            q1, q2, *state = carried
            q0, x = queries.at(slot, u), gated_ref[c, k]
            gate_ref[c, k] = taps[0] * q0 + taps[1] * q1 + taps[2] * q2
            state = [d * s + x for d, s in zip(decay, state)]
            conv_ref[c, k] = total([a * s for a, s in zip(coef, state)] + [skip * x])
            return (q0, q1, *state)

        chunk_loop(steps, one, spreading((queries,)), (*before, *[start_ref[c, n] for n in range(modes)]))
        return 0

    lax.fori_loop(0, beside, group, 0)


def carry_kernel(conv_ref, gate_ref, rate_ref, decay_ref, enter_ref, out_ref, mixed, slots, sem):
    groups, steps = conv_ref.shape[:2]
    modes, chunks = rate_ref.shape[0], steps // CHUNK

    def store(c, side):
        return pltpu.make_async_copy(mixed.at[side], out_ref.at[:, lanes(c)], sem.at[side])

    def group(c, _):
        side, on = lax.rem(c, 2), lanes(c)

        @pl.when(c >= 2)
        def _():
            store(c - 2, side).wait()

        row = pl.ds(c, 1)
        decay = each(decay_ref, on)
        first = lax.broadcasted_iota(jnp.int32, (SEG, LANES), 0).astype(f32) * steps
        part = [jnp.exp(-rows(rate_ref[n : n + 1, on]) * first) * rows(enter_ref[n, row, :]) for n in range(modes)]

        def one(k, slot, u, part):
            part = [d * s for d, s in zip(decay, part)]
            slots[slot, pl.ds(u, SEG, stride=PITCH), :] = gate_ref[c, k] * (conv_ref[c, k] + total(part))
            return part

        def put(seg, chunk, slot, tile):
            start = pl.multiple_of(seg * steps + chunk * CHUNK + tile * TILE, TILE)
            mixed[side, pl.ds(start, TILE), :] = slots[slot, pl.ds(seg * PITCH + tile * TILE, TILE), :]

        items = [(seg, tile) for tile in range(CHUNK // TILE) for seg in range(SEG)]

        def ahead(u, b, coming, after):
            for seg, tile in items[u * len(items) // CHUNK : (u + 1) * len(items) // CHUNK]:
                put(seg, jnp.maximum(b - 1, 0), after, tile)

        chunk_loop(steps, one, ahead, part)
        for seg, tile in items:
            put(seg, chunks - 1, (chunks - 1) % 2, tile)

        for t in range(2):
            gate = gate_ref[c, t, 0:1, :] + enter_ref[modes + 2 + t, row, :]
            mixed[side, t : t + 1, :] = gate * (conv_ref[c, t, 0:1, :] + enter_ref[modes + t, row, :])
        store(c, side).start()
        return 0

    lax.fori_loop(0, groups, group, 0)
    for c in range(max(groups - 2, 0), groups):
        store(c, c % 2).wait()


def in_hbm(x):
    return pltpu.with_memory_space_constraint(x, pltpu.HBM)


def windows(groups, rounds):
    counts = [0] * rounds
    order = [*range(1, rounds), 0]
    for i in range(groups):
        counts[order[i % rounds] if i < rounds else 1 + (i - rounds) % (rounds - 1)] += 1
    return counts


def body(streams, short_filter, residues, rates, skip):
    tokens, _, channels = streams.shape
    modes = rates.shape[0]
    steps = tokens // SEG
    groups = channels // LANES
    count = lax.axis_size("seq")
    assert count & (count - 1) == 0 and tokens % (SEG * CHUNK * 2) == 0

    by_stream = in_hbm(jnp.transpose(streams, (1, 0, 2)))
    apart = lax.optimization_barrier(rates)
    coefficient = lax.optimization_barrier(residues * jnp.sqrt(-jnp.expm1(-2.0 * apart)))
    coefficient = coefficient.reshape(modes, groups, LANES)
    skip = skip.reshape(1, groups, LANES)

    segs = pltpu.VMEM((groups, steps, SEG, LANES), f32)
    spread = pltpu.VMEM((2, SEG * CHUNK, LANES), f32)
    slots = pltpu.VMEM((2, SEG * PITCH, LANES), f32)
    hbm = pl.BlockSpec(memory_space=pltpu.HBM)
    whole = pl.BlockSpec(memory_space=pltpu.VMEM)
    params = pltpu.CompilerParams(vmem_limit_bytes=VMEM_LIMIT)

    def tall(count):
        return pltpu.VMEM((count, groups, LANES), f32)

    enter_shape = tall(modes + 4 + HEAD)
    mode_shape = pltpu.VMEM((modes, channels), f32)

    gated, starts, block, query, taps, tall_taps, tall_rate, rate, decay, entering = pl.pallas_call(
        states_kernel,
        in_specs=[hbm] * 3,
        out_specs=[whole] * 10,
        out_shape=[
            segs,
            pltpu.VMEM((groups, modes, SEG, LANES), f32),
            tall(modes + RIM + HEAD),
            pltpu.VMEM((groups, tokens, LANES), streams.dtype),
            pltpu.VMEM(short_filter.shape, f32),
            tall(9),
            tall(modes),
            mode_shape,
            mode_shape,
            enter_shape,
        ],
        scratch_shapes=[
            pltpu.VMEM((2, 2, tokens, LANES), streams.dtype),
            mode_shape,
            spread,
            spread,
            pltpu.SemaphoreType.DMA((2,)),
            pltpu.SemaphoreType.DMA((groups,)),
            pltpu.SemaphoreType.DMA((2,)),
        ],
        compiler_params=params,
        name="states",
    )(by_stream, in_hbm(short_filter), in_hbm(rates))

    rounds = count.bit_length() - 1
    made, at = (), 0
    for r, beside in enumerate(windows(groups, rounds)):
        size = 1 << r
        other = lax.ppermute(block, "seq", [(i, i ^ size) for i in range(count)])
        if beside:
            inputs = [query, gated, taps, decay, coefficient, skip, starts]
            made = pl.pallas_call(
                functools.partial(local_kernel, at, beside),
                in_specs=[whole] * len(inputs) + [whole] * len(made),
                out_specs=[whole] * 2,
                out_shape=[segs, segs],
                input_output_aliases={len(inputs) + i: i for i in range(len(made))},
                scratch_shapes=[spread],
                compiler_params=params,
                name="local",
            )(*inputs, *made)
            at += beside
        last = r == rounds - 1
        sent = tall(modes + RIM + (0 if r == rounds - 2 else HEAD))
        entering, *blocks = pl.pallas_call(
            functools.partial(join_kernel, size, tokens, last),
            in_specs=[whole] * 7,
            out_specs=[whole] * (1 if last else 2),
            out_shape=[enter_shape] if last else [enter_shape, sent],
            compiler_params=params,
            name="join",
        )(tall_taps, tall_rate, coefficient, skip, other, block, entering)
        block = None if last else blocks[0]
    conv, gate = made

    return pl.pallas_call(
        carry_kernel,
        in_specs=[whole] * 5,
        out_specs=hbm,
        out_shape=pltpu.HBM((tokens, channels), f32),
        scratch_shapes=[pltpu.VMEM((2, tokens, LANES), f32), slots, pltpu.SemaphoreType.DMA((2,))],
        compiler_params=params,
        name="carry",
    )(conv, gate, rate, decay, entering)


def solution(mesh):
    placed = (P(("groups", "seq"), None, None), P(), P(), P(), P())

    return jax.shard_map(body, mesh=mesh, in_specs=placed, out_specs=P(("groups", "seq"), None), check_vma=False)
```

```python
import functools

import jax
import jax.numpy as jnp
from jax import lax
from jax.experimental import pallas as pl
from jax.experimental.pallas import tpu as pltpu
from jax.sharding import PartitionSpec as P


SEG = 8
LANES = 128
CHUNK = 16
RIM, HEAD = 6, 4
PITCH = CHUNK + 8
VMEM_LIMIT = 20 << 20
f32 = jnp.float32


def rows(vec):
    return jnp.broadcast_to(vec, (SEG, LANES))


def total(parts):
    while len(parts) > 1:
        tail = [parts[-1]] if len(parts) % 2 else []
        parts = [a + b for a, b in zip(parts[::2], parts[1::2])] + tail
    return parts[0]


def later(x, by):
    row = lax.broadcasted_iota(jnp.int32, x.shape, 0)
    return jnp.where(row >= by, pltpu.roll(x, by, 0), 0.0)


def each(ref, at):
    return [rows(ref[n : n + 1, at]) for n in range(ref.shape[0])]


class Spread:
    def __init__(self, block, group, buffers, steps):
        self.block, self.group, self.buffers, self.steps = block, group, buffers, steps

    def load(self, seg, chunk, side, first=0, group=None):
        start = pl.multiple_of(seg * self.steps + chunk * CHUNK, CHUNK)
        on = lanes(self.group if group is None else group)
        piece = self.block[pl.ds(start, CHUNK), on].astype(f32)[first:]
        self.buffers[side][pl.ds(first * SEG + seg, CHUNK - first, stride=SEG), :] = piece

    def at(self, side, k):
        return self.buffers[side][pl.ds(k * SEG, SEG), :]

    def begin(self):
        for seg in range(SEG):
            self.load(seg, 0, 0)

    def before(self):
        for seg in range(SEG):
            self.load(seg, self.steps // CHUNK - 1, 1, CHUNK - 2)
        return later(self.at(1, CHUNK - 1), 1), later(self.at(1, CHUNK - 2), 1)


def chunk_loop(steps, one, ahead, items, start, begin=0, end=None, first=None):
    def trip(b, c):
        if first is not None:
            first(b)
        for side in range(2):
            for u in range(CHUNK):
                c = one((2 * b + side) * CHUNK + u, side, u, c)
                for item in items[u * len(items) // CHUNK : (u + 1) * len(items) // CHUNK]:
                    ahead(*item, 2 * b + side, 1 - side)
        return c

    return lax.fori_loop(begin, steps // (2 * CHUNK) if end is None else end, trip, start)


def lanes(c):
    return pl.ds(pl.multiple_of(c * LANES, LANES) if not isinstance(c, int) else c * LANES, LANES)


def states_kernel(
    stream_ref, tap_ref, rate_ref,
    gated_ref, start_ref, send_ref, query_ref, taps_ref, tall_taps, tall_rates, rates_ref, decay_ref, enter_ref,
    raw, stride_decay, *rest,
):
    buffers, (raw_sem, query_sem, small_sem) = (rest[:2], rest[2:4]), rest[4:]
    groups, steps = gated_ref.shape[:2]
    modes, tokens, chunks = rate_ref.shape[0], steps * SEG, steps // CHUNK

    edges = [0, *[1 << i for i in range(groups.bit_length())]]
    edges = [*[e for e in edges if e < groups], groups]
    fetches = []
    for i, (begin, end) in enumerate(zip(edges, edges[1:])):
        on = pl.ds(begin * LANES, (end - begin) * LANES)
        fetches.append(pltpu.make_async_copy(stream_ref.at[1:3, :, on], raw.at[:, :, on], raw_sem.at[i]))
    fetch_query = pltpu.make_async_copy(stream_ref.at[0], query_ref, query_sem)

    def spreads(c):
        return [Spread(raw.at[j], c, buffers[j], steps) for j in range(2)]

    small = [
        pltpu.make_async_copy(rate_ref, rates_ref, small_sem.at[0]),
        pltpu.make_async_copy(tap_ref, taps_ref, small_sem.at[1]),
    ]
    fetches[0].start()
    for copy in (*small, *fetches[1:], fetch_query):
        copy.start()
    for copy in small:
        copy.wait()
    decay_ref[...] = jnp.exp(-rates_ref[...])
    stride_decay[...] = jnp.exp(-rates_ref[...] * float(steps))
    enter_ref[...] = jnp.zeros_like(enter_ref)

    fetches[0].wait()
    for part in spreads(0):
        part.begin()

    def group(c, _):
        def next_landed(b):
            for begin, copy in zip(edges[1:-1], fetches[1:]):

                @pl.when((b + 1 == chunks // 2) & (c + 1 == begin))
                def _():
                    copy.wait()

        parts = keys, vals = spreads(c)
        at, row = lanes(c), pl.ds(c, 1)
        taps = [[rows(taps_ref[d, j : j + 1, at]) for d in range(3)] for j in (1, 2)]
        decay = each(decay_ref, at)
        before = [*keys.before(), *vals.before()]

        def one(k, side, u, carried):
            k1, k2, v1, v2, *state = carried
            k0, v0 = keys.at(side, u), vals.at(side, u)
            a = taps[0][0] * k0 + taps[0][1] * k1 + taps[0][2] * k2
            b = taps[1][0] * v0 + taps[1][1] * v1 + taps[1][2] * v2
            x = a * b
            gated_ref[c, k] = x
            return (k0, k1, v0, v1, *[d * s + x for d, s in zip(decay, state)])

        def ahead(j, seg, chunk, side):
            group = jnp.where(chunk + 1 == chunks, lax.rem(c + 1, groups), c) if side == 0 else None
            parts[j].load(seg, lax.rem(chunk + 1, chunks), side, group=group)

        zero = jnp.zeros((SEG, LANES), f32)
        items = [(j, seg) for seg in range(SEG) for j in range(2)]
        final = chunk_loop(steps, one, ahead, items, (*before, *[zero] * modes), first=next_landed)[4:]
        for n, d in enumerate(each(stride_decay, at)):
            s = final[n]
            for by in (1, 2, 4):
                s = s + d * later(s, by)
                d = d * d
            start_ref[c, n] = later(s, 1)
            send_ref[n, row, :] = s[SEG - 1 : SEG, :]
            tall_rates[n, row, :] = rates_ref[n : n + 1, at]
        for j in range(3):
            for d in range(3):
                tall_taps[3 * j + d, row, :] = taps_ref[d, j : j + 1, at]
        for j in range(2):
            rim = raw[j, tokens - CHUNK :, at].astype(f32)[CHUNK - 2 :]
            head = raw[j, :CHUNK, at].astype(f32)[:2]
            for t in range(2):
                send_ref[modes + 2 * j + t, row, :] = rim[t : t + 1]
                send_ref[modes + RIM + 2 * j + t, row, :] = head[t : t + 1]
                enter_ref[modes + 4 + 2 * j + t, row, :] = head[t : t + 1]
        return 0

    lax.fori_loop(0, groups, group, 0)

    fetch_query.wait()
    for c in range(groups):
        rim = query_ref[tokens - CHUNK :, lanes(c)].astype(f32)[CHUNK - 2 :]
        for t in range(2):
            send_ref[modes + 4 + t, c : c + 1, :] = rim[t : t + 1]


def join_kernel(size, tokens, last, tap_ref, rate_ref, coef_ref, skip_ref, other_ref, mine_ref, enter_ref, enter_out, *mine_out):
    modes = rate_ref.shape[0]
    rim_at, change_at, head_at = modes, modes, modes + 4
    place = lax.axis_index("seq")
    second = (place & size) != 0
    rate = rate_ref[...]

    def after(times):
        return jnp.exp(-rate * times)

    def change(rim, head):
        w = [[tap_ref[3 * j + d] for d in range(3)] for j in (1, 2, 0)]
        more0 = [w[j][1] * rim[2 * j + 1] + w[j][2] * rim[2 * j] for j in range(3)]
        more1 = [w[j][2] * rim[2 * j + 1] for j in range(3)]
        own0 = [w[j][0] * head[2 * j] for j in range(2)]
        own1 = [w[j][0] * head[2 * j + 1] + w[j][1] * head[2 * j] for j in range(2)]
        change0 = (own0[0] + more0[0]) * (own0[1] + more0[1]) - own0[0] * own0[1]
        change1 = (own1[0] + more1[0]) * (own1[1] + more1[1]) - own1[0] * own1[1]
        return change0, change1, more0[2], more1[2]

    def merge(early, late, change0, change1, head_ref, head_from):
        span = float(tokens * size)
        out = mine_out[0]
        out[:modes] = late[:modes] + after(span) * early[:modes] + after(span - 1.0) * change0 + after(span - 2.0) * change1
        out[rim_at : rim_at + RIM] = late[rim_at : rim_at + RIM]
        head = head_ref[head_from : head_from + HEAD]
        enter_out[head_at : head_at + HEAD] = head
        if out.shape[0] > modes + RIM:
            out[rim_at + RIM :] = head

    @pl.when(second)
    def _():
        edge = change(other_ref[rim_at : rim_at + RIM], enter_ref[head_at : head_at + HEAD])
        before = place & (size - 1)
        span = before.astype(f32) * float(tokens)
        enter_out[:modes] = (
            enter_ref[:modes] + after(span) * other_ref[:modes] + after(span - 1.0) * edge[0] + after(span - 2.0) * edge[1]
        )
        enter_out[change_at:] = enter_ref[change_at:]

        @pl.when(before == 0)
        def _():
            for i, row in enumerate(edge):
                enter_out[change_at + i] = row

        if not last:
            merge(other_ref, mine_ref, *edge[:2], other_ref, rim_at + RIM)

    @pl.when(jnp.logical_not(second))
    def _():
        enter_out[...] = enter_ref[...]
        if not last:
            edge = change(mine_ref[rim_at : rim_at + RIM], other_ref[rim_at + RIM : rim_at + RIM + HEAD])
            merge(mine_ref, other_ref, *edge[:2], enter_ref, head_at)

    if last:
        coef, skip = coef_ref[...], skip_ref[0]
        weight = coef * enter_out[:modes]
        change0, change1 = enter_out[change_at], enter_out[change_at + 1]
        once = after(1.0)
        enter_out[:modes] = weight
        enter_out[change_at] = skip * change0 + jnp.sum(weight * once - coef * (after(-1.0) * change1), axis=0)
        enter_out[change_at + 1] = skip * change1 + jnp.sum(weight * (once * once), axis=0)


def local_kernel(at, beside, query_ref, gated_ref, tap_ref, decay_ref, coef_ref, skip_ref, start_ref, *rest):
    conv_ref, gate_ref, *buffers = rest[-4:]
    steps = gated_ref.shape[1]
    modes, chunks = decay_ref.shape[0], steps // CHUNK

    def group(i, _):
        c = i + at
        on = lanes(c)
        queries = Spread(query_ref, c, buffers, steps)
        taps = [rows(tap_ref[d, 0:1, on]) for d in range(3)]
        decay = each(decay_ref, on)
        coef = [rows(coef_ref[n, pl.ds(c, 1), :]) for n in range(modes)]
        skip = rows(skip_ref[0, pl.ds(c, 1), :])
        queries.begin()
        before = queries.before()

        def one(k, side, u, carried):
            q1, q2, *state = carried
            q0, x = queries.at(side, u), gated_ref[c, k]
            gate_ref[c, k] = taps[0] * q0 + taps[1] * q1 + taps[2] * q2
            state = [d * s + x for d, s in zip(decay, state)]
            conv_ref[c, k] = total([a * s for a, s in zip(coef, state)] + [skip * x])
            return (q0, q1, *state)

        def ahead(seg, chunk, side):
            queries.load(seg, lax.rem(chunk + 1, chunks), side)

        items = [(seg,) for seg in range(SEG)]
        chunk_loop(steps, one, ahead, items, (*before, *[start_ref[c, n] for n in range(modes)]))
        return 0

    lax.fori_loop(0, beside, group, 0)


def carry_kernel(conv_ref, gate_ref, rate_ref, decay_ref, enter_ref, out_ref, mixed, *rest):
    buffers, sem = rest[:2], rest[2]
    groups, steps = conv_ref.shape[:2]
    modes = rate_ref.shape[0]
    quarter = steps // 4

    def store(c, side, part):
        here = pl.ds(part * quarter, quarter)
        return pltpu.make_async_copy(mixed.at[side, :, here, :], out_ref.at[:, here, lanes(c)], sem.at[side, part])

    def group(c, _):
        half, on = lax.rem(c, 2), lanes(c)

        @pl.when(c >= 2)
        def _():
            for part in range(4):
                store(c - 2, half, part).wait()

        row = pl.ds(c, 1)
        decay = each(decay_ref, on)
        first = lax.broadcasted_iota(jnp.int32, (SEG, LANES), 0).astype(f32) * steps
        start = [jnp.exp(-rows(rate_ref[n : n + 1, on]) * first) * rows(enter_ref[n, row, :]) for n in range(modes)]

        def one(k, side, u, part):
            part = [d * s for d, s in zip(decay, part)]
            buffers[side][pl.ds(u, SEG, stride=PITCH), :] = gate_ref[c, k] * (conv_ref[c, k] + total(part))
            return part

        def put(seg, chunk, side):
            to = pl.ds(pl.multiple_of(chunk * CHUNK, CHUNK), CHUNK)
            mixed[half, seg, to, :] = buffers[side][pl.ds(seg * PITCH, CHUNK), :]

        def ahead(seg, chunk, side):
            if side == 0:
                put(seg, chunk - 1, side)

        items = [(seg,) for seg in range(SEG)]
        for part in range(4):
            begin, end = part * quarter // (2 * CHUNK), (part + 1) * quarter // (2 * CHUNK)
            start = chunk_loop(steps, one, ahead, items, start, begin, end)
            for seg in range(SEG):
                put(seg, 2 * end - 1, 1)
            assert end == begin + 1
            if part == 0:
                for t in range(2):
                    gate = gate_ref[c, t, 0:1, :] + enter_ref[modes + 2 + t, row, :]
                    local = conv_ref[c, t, 0:1, :] + enter_ref[modes + t, row, :]
                    mixed[half, 0, t : t + 1, :] = gate * local
            store(c, half, part).start()
        return 0

    lax.fori_loop(0, groups, group, 0)
    for c in range(max(groups - 2, 0), groups):
        for part in range(4):
            store(c, c % 2, part).wait()


def in_hbm(x):
    return pltpu.with_memory_space_constraint(x, pltpu.HBM)


def windows(groups, rounds):
    counts = [0] * rounds
    order = [*range(1, rounds), 0]
    for i in range(groups):
        counts[order[i % rounds] if i < rounds else 1 + (i - rounds) % (rounds - 1)] += 1
    return counts


def body(streams, short_filter, residues, rates, skip):
    tokens, _, channels = streams.shape
    modes = rates.shape[0]
    steps = tokens // SEG
    groups = channels // LANES
    count = lax.axis_size("seq")
    assert count & (count - 1) == 0 and tokens % (SEG * CHUNK * 8) == 0

    by_stream = in_hbm(jnp.transpose(streams, (1, 0, 2)))
    apart = lax.optimization_barrier(rates)
    coefficient = lax.optimization_barrier(residues * jnp.sqrt(-jnp.expm1(-2.0 * apart)))
    coefficient = coefficient.reshape(modes, groups, LANES)
    skip = skip.reshape(1, groups, LANES)

    segs = pltpu.VMEM((groups, steps, SEG, LANES), f32)
    spread = [pltpu.VMEM((SEG * CHUNK, LANES), f32)] * 2
    gather = [pltpu.VMEM((SEG * PITCH, LANES), f32)] * 2
    hbm = pl.BlockSpec(memory_space=pltpu.HBM)
    whole = pl.BlockSpec(memory_space=pltpu.VMEM)
    params = pltpu.CompilerParams(vmem_limit_bytes=VMEM_LIMIT)

    def tall(count):
        return pltpu.VMEM((count, groups, LANES), f32)

    enter_shape = tall(modes + 4 + HEAD)
    mode_shape = pltpu.VMEM((modes, channels), f32)

    gated, starts, block, query, taps, tall_taps, tall_rate, rate, decay, entering = pl.pallas_call(
        states_kernel,
        in_specs=[hbm] * 3,
        out_specs=[whole] * 10,
        out_shape=[
            segs,
            pltpu.VMEM((groups, modes, SEG, LANES), f32),
            tall(modes + RIM + HEAD),
            pltpu.VMEM((tokens, channels), streams.dtype),
            pltpu.VMEM(short_filter.shape, f32),
            tall(9),
            tall(modes),
            mode_shape,
            mode_shape,
            enter_shape,
        ],
        scratch_shapes=[
            pltpu.VMEM((2, tokens, channels), streams.dtype),
            mode_shape,
            *spread,
            *spread,
            pltpu.SemaphoreType.DMA((groups.bit_length(),)),
            pltpu.SemaphoreType.DMA,
            pltpu.SemaphoreType.DMA((2,)),
        ],
        compiler_params=params,
        name="states",
    )(by_stream, in_hbm(short_filter), in_hbm(rates))

    rounds = count.bit_length() - 1
    made, at = (), 0
    for r, beside in enumerate(windows(groups, rounds)):
        size = 1 << r
        other = lax.ppermute(block, "seq", [(i, i ^ size) for i in range(count)])
        if beside:
            inputs = [query, gated, taps, decay, coefficient, skip, starts]
            made = pl.pallas_call(
                functools.partial(local_kernel, at, beside),
                in_specs=[whole] * len(inputs) + [whole] * len(made),
                out_specs=[whole] * 2,
                out_shape=[segs, segs],
                input_output_aliases={len(inputs) + i: i for i in range(len(made))},
                scratch_shapes=spread,
                compiler_params=params,
                name="local",
            )(*inputs, *made)
            at += beside
        last = r == rounds - 1
        sent = tall(modes + RIM + (0 if r == rounds - 2 else HEAD))
        entering, *blocks = pl.pallas_call(
            functools.partial(join_kernel, size, tokens, last),
            in_specs=[whole] * 7,
            out_specs=[whole] * (1 if last else 2),
            out_shape=[enter_shape] if last else [enter_shape, sent],
            compiler_params=params,
            name="join",
        )(tall_taps, tall_rate, coefficient, skip, other, block, entering)
        block = None if last else blocks[0]
    conv, gate = made

    mixed = pl.pallas_call(
        carry_kernel,
        in_specs=[whole] * 5,
        out_specs=hbm,
        out_shape=pltpu.HBM((SEG, steps, channels), f32),
        scratch_shapes=[pltpu.VMEM((2, SEG, steps, LANES), f32), *gather, pltpu.SemaphoreType.DMA((2, 4))],
        compiler_params=params,
        name="carry",
    )(conv, gate, rate, decay, entering)
    return mixed.reshape(tokens, channels)


def solution(mesh):
    placed = (P(("groups", "seq"), None, None), P(), P(), P(), P())

    return jax.shard_map(body, mesh=mesh, in_specs=placed, out_specs=P(("groups", "seq"), None), check_vma=False)
```

```python
import functools

import jax
import jax.numpy as jnp
from jax import lax
from jax.experimental import pallas as pl
from jax.experimental.pallas import tpu as pltpu
from jax.sharding import PartitionSpec as P


SEG = 8
LANES = 128
CHUNK = 16
RIM, HEAD = 6, 4
PITCH = CHUNK + 8
VMEM_LIMIT = 20 << 20
f32 = jnp.float32


def rows(vec):
    return jnp.broadcast_to(vec, (SEG, LANES))


def total(parts):
    while len(parts) > 1:
        tail = [parts[-1]] if len(parts) % 2 else []
        parts = [a + b for a, b in zip(parts[::2], parts[1::2])] + tail
    return parts[0]


def later(x, by):
    row = lax.broadcasted_iota(jnp.int32, x.shape, 0)
    return jnp.where(row >= by, pltpu.roll(x, by, 0), 0.0)


def each(ref, at):
    return [rows(ref[n : n + 1, at]) for n in range(ref.shape[0])]


class Spread:
    def __init__(self, block, group, buffers, steps):
        self.block, self.group, self.buffers, self.steps = block, group, buffers, steps

    def load(self, seg, chunk, side, first=0, group=None):
        start = pl.multiple_of(seg * self.steps + chunk * CHUNK, CHUNK)
        on = lanes(self.group if group is None else group)
        piece = self.block[pl.ds(start, CHUNK), on].astype(f32)[first:]
        self.buffers[side][pl.ds(first * SEG + seg, CHUNK - first, stride=SEG), :] = piece

    def at(self, side, k):
        return self.buffers[side][pl.ds(k * SEG, SEG), :]

    def begin(self):
        for seg in range(SEG):
            self.load(seg, 0, 0)

    def before(self):
        for seg in range(SEG):
            self.load(seg, self.steps // CHUNK - 1, 1, CHUNK - 2)
        return later(self.at(1, CHUNK - 1), 1), later(self.at(1, CHUNK - 2), 1)


def chunk_loop(steps, one, ahead, items, start, begin=0, end=None, first=None):
    def trip(b, c):
        if first is not None:
            first(b)
        for side in range(2):
            for u in range(CHUNK):
                c = one((2 * b + side) * CHUNK + u, side, u, c)
                for item in items[u * len(items) // CHUNK : (u + 1) * len(items) // CHUNK]:
                    ahead(*item, 2 * b + side, 1 - side)
        return c

    return lax.fori_loop(begin, steps // (2 * CHUNK) if end is None else end, trip, start)


def lanes(c):
    return pl.ds(pl.multiple_of(c * LANES, LANES) if not isinstance(c, int) else c * LANES, LANES)


def states_kernel(
    stream_ref, tap_ref, rate_ref,
    gated_ref, start_ref, send_ref, query_ref, taps_ref, tall_taps, tall_rates, rates_ref, decay_ref, enter_ref,
    raw, stride_decay, *rest,
):
    buffers, (raw_sem, query_sem, small_sem) = (rest[:2], rest[2:4]), rest[4:]
    groups, steps = gated_ref.shape[:2]
    modes, tokens, chunks = rate_ref.shape[0], steps * SEG, steps // CHUNK

    edges = [0, *[1 << i for i in range(groups.bit_length())]]
    edges = [*[e for e in edges if e < groups], groups]
    fetches = []
    for i, (begin, end) in enumerate(zip(edges, edges[1:])):
        on = pl.ds(begin * LANES, (end - begin) * LANES)
        fetches.append(pltpu.make_async_copy(stream_ref.at[1:3, :, on], raw.at[:, :, on], raw_sem.at[i]))
    fetch_query = pltpu.make_async_copy(stream_ref.at[0], query_ref, query_sem)

    def spreads(c):
        return [Spread(raw.at[j], c, buffers[j], steps) for j in range(2)]

    small = [
        pltpu.make_async_copy(rate_ref, rates_ref, small_sem.at[0]),
        pltpu.make_async_copy(tap_ref, taps_ref, small_sem.at[1]),
    ]
    fetches[0].start()
    for copy in (*small, *fetches[1:], fetch_query):
        copy.start()
    for copy in small:
        copy.wait()
    decay_ref[...] = jnp.exp(-rates_ref[...])
    stride_decay[...] = jnp.exp(-rates_ref[...] * float(steps))
    enter_ref[...] = jnp.zeros_like(enter_ref)

    fetches[0].wait()
    for part in spreads(0):
        part.begin()

    def group(c, _):
        def next_landed(b):
            for begin, copy in zip(edges[1:-1], fetches[1:]):

                @pl.when((b + 1 == chunks // 2) & (c + 1 == begin))
                def _():
                    copy.wait()

        parts = keys, vals = spreads(c)
        at, row = lanes(c), pl.ds(c, 1)
        taps = [[rows(taps_ref[d, j : j + 1, at]) for d in range(3)] for j in (1, 2)]
        decay = each(decay_ref, at)
        before = [*keys.before(), *vals.before()]

        def one(k, side, u, carried):
            k1, k2, v1, v2, *state = carried
            k0, v0 = keys.at(side, u), vals.at(side, u)
            a = taps[0][0] * k0 + taps[0][1] * k1 + taps[0][2] * k2
            b = taps[1][0] * v0 + taps[1][1] * v1 + taps[1][2] * v2
            x = a * b
            gated_ref[c, k] = x
            return (k0, k1, v0, v1, *[d * s + x for d, s in zip(decay, state)])

        def ahead(j, seg, chunk, side):
            group = jnp.where(chunk + 1 == chunks, lax.rem(c + 1, groups), c) if side == 0 else None
            parts[j].load(seg, lax.rem(chunk + 1, chunks), side, group=group)

        zero = jnp.zeros((SEG, LANES), f32)
        items = [(j, seg) for seg in range(SEG) for j in range(2)]
        final = chunk_loop(steps, one, ahead, items, (*before, *[zero] * modes), first=next_landed)[4:]
        for n, d in enumerate(each(stride_decay, at)):
            s = final[n]
            for by in (1, 2, 4):
                s = s + d * later(s, by)
                d = d * d
            start_ref[c, n] = later(s, 1)
            send_ref[n, row, :] = s[SEG - 1 : SEG, :]
            tall_rates[n, row, :] = rates_ref[n : n + 1, at]
        for j in range(3):
            for d in range(3):
                tall_taps[3 * j + d, row, :] = taps_ref[d, j : j + 1, at]
        for j in range(2):
            rim = raw[j, tokens - CHUNK :, at].astype(f32)[CHUNK - 2 :]
            head = raw[j, :CHUNK, at].astype(f32)[:2]
            for t in range(2):
                send_ref[modes + 2 * j + t, row, :] = rim[t : t + 1]
                send_ref[modes + RIM + 2 * j + t, row, :] = head[t : t + 1]
                enter_ref[modes + 4 + 2 * j + t, row, :] = head[t : t + 1]
        return 0

    lax.fori_loop(0, groups, group, 0)

    fetch_query.wait()
    for c in range(groups):
        rim = query_ref[tokens - CHUNK :, lanes(c)].astype(f32)[CHUNK - 2 :]
        for t in range(2):
            send_ref[modes + 4 + t, c : c + 1, :] = rim[t : t + 1]


def join_kernel(size, tokens, last, tap_ref, rate_ref, coef_ref, skip_ref, other_ref, mine_ref, enter_ref, enter_out, *mine_out):
    modes = rate_ref.shape[0]
    rim_at, change_at, head_at = modes, modes, modes + 4
    place = lax.axis_index("seq")
    second = (place & size) != 0
    rate = rate_ref[...]

    def after(times):
        return jnp.exp(-rate * times)

    def change(rim, head):
        w = [[tap_ref[3 * j + d] for d in range(3)] for j in (1, 2, 0)]
        more0 = [w[j][1] * rim[2 * j + 1] + w[j][2] * rim[2 * j] for j in range(3)]
        more1 = [w[j][2] * rim[2 * j + 1] for j in range(3)]
        own0 = [w[j][0] * head[2 * j] for j in range(2)]
        own1 = [w[j][0] * head[2 * j + 1] + w[j][1] * head[2 * j] for j in range(2)]
        change0 = (own0[0] + more0[0]) * (own0[1] + more0[1]) - own0[0] * own0[1]
        change1 = (own1[0] + more1[0]) * (own1[1] + more1[1]) - own1[0] * own1[1]
        return change0, change1, more0[2], more1[2]

    def merge(early, late, change0, change1, head_ref, head_from):
        span = float(tokens * size)
        out = mine_out[0]
        out[:modes] = late[:modes] + after(span) * early[:modes] + after(span - 1.0) * change0 + after(span - 2.0) * change1
        out[rim_at : rim_at + RIM] = late[rim_at : rim_at + RIM]
        head = head_ref[head_from : head_from + HEAD]
        enter_out[head_at : head_at + HEAD] = head
        if out.shape[0] > modes + RIM:
            out[rim_at + RIM :] = head

    @pl.when(second)
    def _():
        edge = change(other_ref[rim_at : rim_at + RIM], enter_ref[head_at : head_at + HEAD])
        before = place & (size - 1)
        span = before.astype(f32) * float(tokens)
        enter_out[:modes] = (
            enter_ref[:modes] + after(span) * other_ref[:modes] + after(span - 1.0) * edge[0] + after(span - 2.0) * edge[1]
        )
        enter_out[change_at:] = enter_ref[change_at:]

        @pl.when(before == 0)
        def _():
            for i, row in enumerate(edge):
                enter_out[change_at + i] = row

        if not last:
            merge(other_ref, mine_ref, *edge[:2], other_ref, rim_at + RIM)

    @pl.when(jnp.logical_not(second))
    def _():
        enter_out[...] = enter_ref[...]
        if not last:
            edge = change(mine_ref[rim_at : rim_at + RIM], other_ref[rim_at + RIM : rim_at + RIM + HEAD])
            merge(mine_ref, other_ref, *edge[:2], enter_ref, head_at)

    if last:
        coef, skip = coef_ref[...], skip_ref[0]
        weight = coef * enter_out[:modes]
        change0, change1 = enter_out[change_at], enter_out[change_at + 1]
        once = after(1.0)
        enter_out[:modes] = weight
        enter_out[change_at] = skip * change0 + jnp.sum(weight * once - coef * (after(-1.0) * change1), axis=0)
        enter_out[change_at + 1] = skip * change1 + jnp.sum(weight * (once * once), axis=0)


def local_kernel(at, beside, query_ref, gated_ref, tap_ref, decay_ref, coef_ref, skip_ref, start_ref, *rest):
    conv_ref, gate_ref, *buffers = rest[-4:]
    steps = gated_ref.shape[1]
    modes, chunks = decay_ref.shape[0], steps // CHUNK

    def group(i, _):
        c = i + at
        on = lanes(c)
        queries = Spread(query_ref, c, buffers, steps)
        taps = [rows(tap_ref[d, 0:1, on]) for d in range(3)]
        decay = each(decay_ref, on)
        coef = [rows(coef_ref[n, pl.ds(c, 1), :]) for n in range(modes)]
        skip = rows(skip_ref[0, pl.ds(c, 1), :])
        queries.begin()
        before = queries.before()

        def one(k, side, u, carried):
            q1, q2, *state = carried
            q0, x = queries.at(side, u), gated_ref[c, k]
            gate_ref[c, k] = taps[0] * q0 + taps[1] * q1 + taps[2] * q2
            state = [d * s + x for d, s in zip(decay, state)]
            conv_ref[c, k] = total([a * s for a, s in zip(coef, state)] + [skip * x])
            return (q0, q1, *state)

        def ahead(seg, chunk, side):
            queries.load(seg, lax.rem(chunk + 1, chunks), side)

        items = [(seg,) for seg in range(SEG)]
        chunk_loop(steps, one, ahead, items, (*before, *[start_ref[c, n] for n in range(modes)]))
        return 0

    lax.fori_loop(0, beside, group, 0)


def carry_kernel(conv_ref, gate_ref, rate_ref, decay_ref, enter_ref, out_ref, mixed, *rest):
    buffers, sem = rest[:2], rest[2]
    groups, steps = conv_ref.shape[:2]
    modes = rate_ref.shape[0]
    quarter = steps // 4

    def store(c, side, part):
        here = pl.ds(part * quarter, quarter)
        return pltpu.make_async_copy(mixed.at[side, :, here, :], out_ref.at[:, here, lanes(c)], sem.at[side, part])

    def group(c, _):
        half, on = lax.rem(c, 2), lanes(c)

        @pl.when(c >= 2)
        def _():
            for part in range(4):
                store(c - 2, half, part).wait()

        row = pl.ds(c, 1)
        decay = each(decay_ref, on)
        first = lax.broadcasted_iota(jnp.int32, (SEG, LANES), 0).astype(f32) * steps
        start = [jnp.exp(-rows(rate_ref[n : n + 1, on]) * first) * rows(enter_ref[n, row, :]) for n in range(modes)]

        def one(k, side, u, part):
            part = [d * s for d, s in zip(decay, part)]
            buffers[side][pl.ds(u, SEG, stride=PITCH), :] = gate_ref[c, k] * (conv_ref[c, k] + total(part))
            return part

        def put(seg, chunk, side):
            to = pl.ds(pl.multiple_of(chunk * CHUNK, CHUNK), CHUNK)
            mixed[half, seg, to, :] = buffers[side][pl.ds(seg * PITCH, CHUNK), :]

        def ahead(seg, chunk, side):
            if side == 0:
                put(seg, chunk - 1, side)

        items = [(seg,) for seg in range(SEG)]
        for part in range(4):
            begin, end = part * quarter // (2 * CHUNK), (part + 1) * quarter // (2 * CHUNK)
            start = chunk_loop(steps, one, ahead, items, start, begin, end)
            for seg in range(SEG):
                put(seg, 2 * end - 1, 1)
            assert end == begin + 1
            if part == 0:
                for t in range(2):
                    gate = gate_ref[c, t, 0:1, :] + enter_ref[modes + 2 + t, row, :]
                    local = conv_ref[c, t, 0:1, :] + enter_ref[modes + t, row, :]
                    mixed[half, 0, t : t + 1, :] = gate * local
            store(c, half, part).start()
        return 0

    lax.fori_loop(0, groups, group, 0)
    for c in range(max(groups - 2, 0), groups):
        for part in range(4):
            store(c, c % 2, part).wait()


def in_hbm(x):
    return pltpu.with_memory_space_constraint(x, pltpu.HBM)


def windows(groups, rounds):
    counts = [(groups + r) // rounds for r in range(rounds)]
    if counts[0] > 1 and rounds > 1:
        counts[0], counts[-1] = counts[0] - 1, counts[-1] + 1
    return counts


def body(streams, short_filter, residues, rates, skip):
    tokens, _, channels = streams.shape
    modes = rates.shape[0]
    steps = tokens // SEG
    groups = channels // LANES
    count = lax.axis_size("seq")
    assert count & (count - 1) == 0 and tokens % (SEG * CHUNK * 8) == 0

    by_stream = in_hbm(jnp.transpose(streams, (1, 0, 2)))
    apart = lax.optimization_barrier(rates)
    coefficient = lax.optimization_barrier(residues * jnp.sqrt(-jnp.expm1(-2.0 * apart)))
    coefficient = coefficient.reshape(modes, groups, LANES)
    skip = skip.reshape(1, groups, LANES)

    segs = pltpu.VMEM((groups, steps, SEG, LANES), f32)
    spread = [pltpu.VMEM((SEG * CHUNK, LANES), f32)] * 2
    gather = [pltpu.VMEM((SEG * PITCH, LANES), f32)] * 2
    hbm = pl.BlockSpec(memory_space=pltpu.HBM)
    whole = pl.BlockSpec(memory_space=pltpu.VMEM)
    params = pltpu.CompilerParams(vmem_limit_bytes=VMEM_LIMIT)

    def tall(count):
        return pltpu.VMEM((count, groups, LANES), f32)

    enter_shape = tall(modes + 4 + HEAD)
    mode_shape = pltpu.VMEM((modes, channels), f32)

    gated, starts, block, query, taps, tall_taps, tall_rate, rate, decay, entering = pl.pallas_call(
        states_kernel,
        in_specs=[hbm] * 3,
        out_specs=[whole] * 10,
        out_shape=[
            segs,
            pltpu.VMEM((groups, modes, SEG, LANES), f32),
            tall(modes + RIM + HEAD),
            pltpu.VMEM((tokens, channels), streams.dtype),
            pltpu.VMEM(short_filter.shape, f32),
            tall(9),
            tall(modes),
            mode_shape,
            mode_shape,
            enter_shape,
        ],
        scratch_shapes=[
            pltpu.VMEM((2, tokens, channels), streams.dtype),
            mode_shape,
            *spread,
            *spread,
            pltpu.SemaphoreType.DMA((groups.bit_length(),)),
            pltpu.SemaphoreType.DMA,
            pltpu.SemaphoreType.DMA((2,)),
        ],
        compiler_params=params,
        name="states",
    )(by_stream, in_hbm(short_filter), in_hbm(rates))

    rounds = count.bit_length() - 1
    made, at = (), 0
    for r, beside in enumerate(windows(groups, rounds)):
        size = 1 << r
        other = lax.ppermute(block, "seq", [(i, i ^ size) for i in range(count)])
        if beside:
            inputs = [query, gated, taps, decay, coefficient, skip, starts]
            made = pl.pallas_call(
                functools.partial(local_kernel, at, beside),
                in_specs=[whole] * len(inputs) + [whole] * len(made),
                out_specs=[whole] * 2,
                out_shape=[segs, segs],
                input_output_aliases={len(inputs) + i: i for i in range(len(made))},
                scratch_shapes=spread,
                compiler_params=params,
                name="local",
            )(*inputs, *made)
            at += beside
        last = r == rounds - 1
        sent = tall(modes + RIM + (0 if r == rounds - 2 else HEAD))
        entering, *blocks = pl.pallas_call(
            functools.partial(join_kernel, size, tokens, last),
            in_specs=[whole] * 7,
            out_specs=[whole] * (1 if last else 2),
            out_shape=[enter_shape] if last else [enter_shape, sent],
            compiler_params=params,
            name="join",
        )(tall_taps, tall_rate, coefficient, skip, other, block, entering)
        block = None if last else blocks[0]
    conv, gate = made

    mixed = pl.pallas_call(
        carry_kernel,
        in_specs=[whole] * 5,
        out_specs=hbm,
        out_shape=pltpu.HBM((SEG, steps, channels), f32),
        scratch_shapes=[pltpu.VMEM((2, SEG, steps, LANES), f32), *gather, pltpu.SemaphoreType.DMA((2, 4))],
        compiler_params=params,
        name="carry",
    )(conv, gate, rate, decay, entering)
    return mixed.reshape(tokens, channels)


def solution(mesh):
    placed = (P(("groups", "seq"), None, None), P(), P(), P(), P())

    return jax.shard_map(body, mesh=mesh, in_specs=placed, out_specs=P(("groups", "seq"), None), check_vma=False)
```
